32 devices in a mesh: row: 4 (over y, x), col: 2 (over core), depth: 4 (over z).
Axes of the slice: x: 2, y: 2, z: 4, core: 2. Of those that a mesh axis runs over, the one named last changes fastest.
Arguments:
- source_desc: bfloat16 [2048, 256], P(('row', 'col', 'depth')), may hold values from -4 to 4
- target_desc: bfloat16 [16384, 256], P(('col', 'depth', 'row')), may hold values from -4 to 4
- target_dual: float32 [16384], P(('col', 'depth')), may hold values from -2 to 4.25
- row_weight: float32 [2048], P('row'), may hold values from 0.3 to 3
- matches: int32 [2048], P('row'), may hold values from 0 to 16383
Outputs:
- grad_source: float32 [2048, 256], P(('row', 'col', 'depth'))
- grad_target: float32 [16384, 256], P(('col', 'depth', 'row'))
The draws below stay inside these ranges and needn't reach their ends.
All inputs are finite; a program needn't handle non-finite values.
Results may differ from the reference program's by a relative error of at most 0.0029.
Values may be sent and summed in bfloat16 or wider, within the bound.
A program may use at most 64 MiB of HBM per device.

```python
import math
import jax
import jax.numpy as jnp
from jax import lax

D = 256
NS = 2048
NT = 16384


def base_desc(key, row_total):
    values = jax.random.normal(jax.random.fold_in(key, 2), (row_total, D), jnp.float32)
    return jnp.clip(values, -4.0, 4.0)


def draw_source_desc(key, part):
    values = base_desc(jax.random.fold_in(key, 11), NS)
    return values.astype(jnp.bfloat16)


def draw_target_desc(key, part):
    values = base_desc(jax.random.fold_in(key, 12), NT)
    return values.astype(jnp.bfloat16)


def draw_target_dual(key, part):
    position = jnp.arange(NT, dtype=jnp.float32) / NT
    jitter = jax.random.uniform(jax.random.fold_in(key, 21), (NT,), minval=-2.0, maxval=2.0)
    return jitter + 1.0986123 * position


def set_ends(drawn, own_key, low, largest):
    dims = drawn.shape
    place = [jax.random.randint(jax.random.fold_in(own_key, axis), (), 0, dims[axis]) for axis in range(len(dims))]
    drawn = drawn.at[tuple(place)].set(low)
    longest = dims.index(max(dims))
    place[longest] = (place[longest] + 1) % dims[longest]
    return drawn.at[tuple(place)].set(largest)


def levels(rng, extent, shards, low, largest):
    gain = 1.0
    for dim, parts in shards:
        heights = jax.random.uniform(jax.random.fold_in(jax.random.fold_in(rng, 6), dim), (parts,), jnp.float32, low / len(shards), largest / len(shards))
        gain = gain * jnp.repeat(jnp.exp(heights), extent[dim] // parts).reshape((-1,) + (1,) * (len(extent) - 1 - dim))
    return gain


def setup_inputs(seed: int = 0) -> dict:
    seeds = jax.random.split(jax.random.key(seed), 6)
    source_desc = draw_source_desc(jax.random.fold_in(seeds[5], 71), 0)
    target_desc = draw_target_desc(jax.random.fold_in(seeds[5], 71), 0)
    target_dual = draw_target_dual(jax.random.fold_in(seeds[5], 71), 0)
    row_weight = jnp.clip(jnp.exp(math.log(3.0) - 2.3025851 * jax.random.uniform(seeds[3], (NS,), jnp.float32) ** levels(seeds[3], (NS,), ((0, 4),), -0.2, 0.2)), 0.3, 3.0)
    matches = set_ends(jax.random.randint(seeds[4], (NS,), 0, NT), jax.random.fold_in(seeds[4], 1), 0, NT - 1).astype(jnp.int32)
    return {"source_desc": source_desc, "target_desc": target_desc, "target_dual": target_dual, "row_weight": row_weight, "matches": matches}


score_scale = 0.1875


def reference(source_desc, target_desc, target_dual, row_weight, matches):
    block_rows = math.gcd(NS, 512)
    columns = jnp.arange(NT, dtype=jnp.int32)

    def advance(tgt_grad, block_idx):
        start = (block_idx * block_rows).astype(jnp.int32)
        src_rows = lax.dynamic_slice_in_dim(source_desc, start, block_rows, 0)
        row_wts = lax.dynamic_slice_in_dim(row_weight, start, block_rows, 0)
        row_match = lax.dynamic_slice_in_dim(matches, start, block_rows, 0)
        scores = score_scale * jnp.dot(src_rows, target_desc.T, preferred_element_type=jnp.float32) + target_dual[None, :]
        highest = jnp.max(scores, axis=1, keepdims=True)
        log_total = highest + jnp.log(jnp.sum(jnp.exp(scores - highest), axis=1, keepdims=True))
        plan_tile = jnp.exp(scores - log_total)
        hit_mask = (columns[None, :] == row_match[:, None]).astype(jnp.float32)
        delta_tile = (row_wts[:, None] * (plan_tile - hit_mask)).astype(jnp.bfloat16)
        src_grad = score_scale * jnp.dot(delta_tile, target_desc, preferred_element_type=jnp.float32)
        tgt_grad = tgt_grad + score_scale * jnp.dot(delta_tile.T, src_rows, preferred_element_type=jnp.float32)
        return tgt_grad, src_grad

    tgt_grad, src_grad = lax.scan(advance, jnp.zeros((NT, D), jnp.float32), jnp.arange(NS // block_rows, dtype=jnp.int32))
    return src_grad.reshape(NS, D), tgt_grad
```

```python
import functools
import jax
import jax.numpy as jnp
from jax import lax
from jax.experimental import pallas as pl
from jax.experimental.pallas import tpu as pltpu
from jax.sharding import PartitionSpec as P

score_scale = 0.1875
F32 = jnp.float32
BF16 = jnp.bfloat16


def kernel(R, NC, ND, src_h, tgt_h, dual_h, weight_h, match_h, gs_out, gt_out,
           tgt, dual_all, weight, match_in, S, Q, QD, T2, dual, dual2, wm, wm_all, wm_g, dcol, e_buf, m_buf, lam,
           dbuf, ps, px, zs, zr, zd, ds, dr, partf, gt_send, gt_recv,
           s_in, s_pair, r_pair, s_z, r_z, s_x, r_x, s_qd, r_qd, s_d, s_wm, r_wm, s_l, r_l, s_p, r_p, s_zp, r_zp,
           s_zd, r_zd, s_dr, r_dr, line_in):
    G = (NC // 2) * ND
    N = R * G
    n, D = src_h.shape
    own = tgt_h.shape[0]
    C = R * n
    row = lax.axis_index("row")
    col = lax.axis_index("col")
    dep = lax.axis_index("depth")
    par = lax.rem(col, 2)
    grp = (col // 2) * ND + dep
    me = grp * R + row
    sib_col = col + 1 - 2 * par
    order = sorted(range(G), key=lambda g: abs(2 * g - G + 1))
    MESH = pl.DeviceIdType.MESH

    def flip(j):
        r, b = row, 1
        while b < R:
            if j & b:
                r = r + b * (1 - 2 * lax.rem(row // b, 2))
            b *= 2
        return r

    if R & (R - 1) == 0:
        rows = [flip(j) for j in range(R)]
    else:
        rows = [lax.rem(row + j, R) for j in range(R)]
    far = R >= 4 and R & (R - 1) == 0
    near = range(1, R - 1) if far else range(1, R)
    rd = rows[R - 1]

    def dev(r, c, d):
        return {"row": r, "col": c, "depth": d}

    sib = dev(row, sib_col, dep)

    def zdev(g):
        return dev(row, (g // ND) * 2 + par, g % ND)

    def zrel(g):
        return dev(row, (g // ND) * 2 + 1 - par, g % ND)

    def xdev(j):
        return dev(rows[j], col, dep)

    def xrel(j):
        return dev(rows[j], sib_col, dep)

    def peer(k):
        i = lax.rem(me + k, N)
        g = i // R
        return dev(lax.rem(i, R), (g // ND) * 2 + par, lax.rem(g, ND))

    def rcopy(a, b, ss, rs, to):
        return pltpu.make_async_remote_copy(src_ref=a, dst_ref=b, send_sem=ss, recv_sem=rs,
                                            device_id=to, device_id_type=MESH)

    def each_peer(fn):
        if N <= 32:
            for g in range(G):
                for j in range(R - 1, 0, -1):
                    fn(dev(rows[j], (g // ND) * 2 + par, g % ND))

                @pl.when(grp != g)
                def _(g=g):
                    fn(zdev(g))
        else:
            lax.fori_loop(1, N, lambda k, c: (fn(peer(k)), c)[1], 0)

    def greet(sem, to):
        pl.semaphore_signal(sem, inc=1, device_id=to, device_id_type=MESH)

    barrier = pltpu.get_barrier_semaphore()
    for g in range(G):
        @pl.when(grp != g)
        def _(g=g):
            greet(barrier, zrel(g))
    for j in near:
        greet(barrier, xdev(j))
        greet(barrier, xrel(j))
    if far:
        greet(barrier, xrel(R - 1))
    greet(barrier, sib)
    loads = [pltpu.make_async_copy(a, b, s_in.at[i]) for i, (a, b) in enumerate((
        (src_h, S.at[grp, row]), (tgt_h, tgt), (dual_h, dual_all), (weight_h, weight), (match_h, match_in)))]
    for c in loads:
        c.start()
    pl.semaphore_wait(barrier, G + 2 * len(near) + (1 if far else 0))

    sends = []

    def go(c):
        c.start()
        sends.append(c)

    mine = src_h

    def z_send(g):
        return rcopy(mine, Q.at[grp], s_z.at[g], r_z.at[grp], zrel(g))

    for g in order:
        @pl.when(grp != g)
        def _(g=g):
            z_send(g).start()
    if far:
        go(rcopy(mine, QD, s_qd, r_qd, xrel(R - 1)))
    for j in near:
        rcopy(mine, S.at[grp, row], s_x.at[j, grp], r_x.at[row, grp], xdev(j)).start()
    go(rcopy(tgt_h, T2, s_pair.at[0], r_pair.at[0], sib))
    for j in range(1, R):
        greet(line_in, xrel(j))
    greet(line_in, sib)
    for c in loads[2:]:
        c.wait()
    dual[...] = dual_all[:, pl.ds(pl.multiple_of(row * own, own), own)]
    go(rcopy(dual, dual2, s_pair.at[1], r_pair.at[1], sib))

    for i, vec in ((0, weight[...]), (1, match_in[...].astype(F32))):
        span = ND * n
        for q in range(2):
            parts = [jnp.where(par == q, vec[:, 2 * c * span:(2 * c + 1) * span],
                               vec[:, (2 * c + 1) * span:(2 * c + 2) * span]) for c in range(NC // 2)]
            wm[q, i:i + 1, :] = parts[0] if len(parts) == 1 else jnp.concatenate(parts, axis=1)
    wm_all[row] = wm[0]
    for j in range(1, R):
        go(rcopy(wm.at[1], wm_all.at[row], s_wm.at[j], r_wm.at[row], xrel(j)))

    def x_send(g, j):
        return rcopy(Q.at[g], S.at[g, row], s_x.at[j, g], r_x.at[row, g], sib if j == 0 else xrel(j))

    def d_send(g):
        return rcopy(QD, S.at[grp, rd], s_d.at[g], r_x.at[rd, grp], zrel(g))

    hops = [0] + list(near)
    if far:
        rcopy(QD, QD, s_qd, r_qd, xrel(R - 1)).wait_recv()
        for g in order:
            d_send(g).start()
    for g in order:
        @pl.when(grp != g)
        def _(g=g):
            rcopy(Q.at[g], Q.at[g], s_z.at[g], r_z.at[g], zrel(g)).wait_recv()
            for j in list(near) + [0]:
                x_send(g, j).start()
    dcol[0:own, :] = jnp.transpose(jnp.broadcast_to(dual[...], (128, own)))
    for c in loads[:2]:
        c.wait()
    rcopy(dual, dual2, s_pair.at[1], r_pair.at[1], sib).wait_recv()
    dcol[own:2 * own, :] = jnp.transpose(jnp.broadcast_to(dual2[...], (128, own)))
    rcopy(tgt, T2, s_pair.at[0], r_pair.at[0], sib).wait_recv()

    lane_rep = C // 128

    def scores_chunk(g):
        block = S[g].reshape(C, D)
        tops = []
        for h, t in ((0, tgt), (1, T2)):
            p = lax.dot_general(t[...], block, (((1,), (1,)), ((), ())), preferred_element_type=F32)
            dc = dcol[h * own:(h + 1) * own, :]
            s = score_scale * p + jnp.concatenate([dc] * lane_rep, axis=1)
            e_buf[g, h * own:(h + 1) * own, :] = s
            tops.append(jnp.max(s, axis=0, keepdims=True))
        top = jnp.maximum(tops[0], tops[1])
        m_buf[g] = top
        e = jnp.exp(e_buf[g] - top)
        e_buf[g] = e
        lam[g, me] = top + jnp.log(jnp.sum(e, axis=0, keepdims=True))

    def take(g, r):
        rcopy(S.at[g, r], S.at[g, r], s_x.at[0, 0], r_x.at[r, g], sib).wait_recv()

    place = sum(i * (grp == g).astype(jnp.int32) for i, g in enumerate(order))
    for i in range(G):
        g = grp if i == 0 else jnp.where(place >= i, order[i - 1], order[i])
        for j in range(0 if i else 1, R):
            take(g, rows[j])
        scores_chunk(g)
        if i == 0:
            pl.semaphore_wait(line_in, R)
        each_peer(lambda to: rcopy(lam.at[g, me], lam.at[g, me], s_l.at[g], r_l.at[g], to).start())

    for j in range(1, R):
        rcopy(wm.at[1], wm_all.at[rows[j]], s_wm.at[j], r_wm.at[rows[j]], xrel(j)).wait_recv()
    for g in range(G):
        for i in range(2):
            wm_g[g, i:i + 1, :] = jnp.concatenate(
                [wm_all[r, i:i + 1, g * n:(g + 1) * n] for r in range(R)], axis=1)

    first = [((c * ND + dep) * R + row) * own for c in (col, sib_col)]

    def lam_all(g):
        every = lam.at[g, pl.ds(0, N - 1)]
        return rcopy(every, every, s_l.at[g], r_l.at[g], sib)

    def delta_chunk(g):
        lam_all(g).wait_recv()
        parts = lam[g]
        peak = jnp.max(parts, axis=0)
        log_total = peak + jnp.log(jnp.sum(jnp.exp(parts - peak[None]), axis=0))
        w = wm_g[g, 0:1, :]
        match = wm_g[g, 1:2, :].astype(jnp.int32)
        scale = w * jnp.exp(m_buf[g] - log_total)
        part = None
        for h, t in ((0, tgt), (1, T2)):
            ids = lax.broadcasted_iota(jnp.int32, (own, C), 0)
            hit = jnp.where(ids == match - first[h], w, 0.0)
            d = (scale * e_buf[g, h * own:(h + 1) * own, :] - hit).astype(BF16)
            dbuf[g, h * own:(h + 1) * own, :] = d
            q = lax.dot_general(d, t[...], (((0,), (0,)), ((), ())), preferred_element_type=F32)
            part = q if part is None else part + q
        return part

    def p_send(g, j):
        apart = (grp != g).astype(jnp.int32)
        to = sib if j == 0 else dev(rows[j], col + apart * (sib_col - col), dep)
        return rcopy(ps.at[g, rows[j]], px.at[g, row], s_p.at[j, g], r_p.at[row, g], to)

    def far_send(g):
        return rcopy(ps.at[g, rd], zd.at[grp], s_zd.at[g], r_zd.at[grp], zrel(g))

    def gt_half(h, groups):
        acc = None
        for g in groups:
            q = jnp.dot(dbuf[g, h * own:(h + 1) * own, :], S[g].reshape(C, D), preferred_element_type=F32)
            acc = q if acc is None else acc + q
        return acc

    for i, g in enumerate(order):
        if i == G - 1 and G > 1:
            gt_send[...] = gt_half(1, order[:-1])
            gt_out[...] = gt_half(0, order[:-1])
        part = delta_chunk(g).reshape(R, n, D)
        ps[g] = part.astype(BF16)
        if far:
            far_send(g).start()
        for j in near:
            p_send(g, j).start()

        @pl.when(grp != g)
        def _(g=g):
            p_send(g, 0).start()

        @pl.when(grp == g)
        def _(part=part):
            partf[...] = part

    last = order[-1:]
    gt_send[...] = gt_send[...] + gt_half(1, last) if G > 1 else gt_half(1, last)
    go(rcopy(gt_send, gt_recv, s_pair.at[2], r_pair.at[2], sib))

    def taken(g, j):
        rcopy(ps.at[g, rows[j]], px.at[g, rows[j]], s_p.at[j, g], r_p.at[rows[j], g], sib).wait_recv()
        return px[g, rows[j]].astype(F32)

    def zp_send(g):
        return rcopy(zs.at[g], zr.at[grp], s_zp.at[g], r_zp.at[grp], zrel(g))

    def relay(g):
        @pl.when(grp != g)
        def _():
            acc = taken(g, 0)
            for j in near:
                acc = acc + taken(g, j)
            zs[g] = acc.astype(BF16)
            zp_send(g).start()

    def far_copy():
        return rcopy(ds, dr, s_dr, r_dr, xrel(R - 1))

    def far_relay():
        acc = None
        for g in range(G):
            rcopy(zs.at[g], zd.at[g], s_zd.at[g], r_zd.at[g], sib).wait_recv()
            acc = zd[g].astype(F32) if acc is None else acc + zd[g].astype(F32)
        ds[...] = acc.astype(BF16)
        far_copy().start()

    for g in order[:-1]:
        relay(g)
    if far:
        pl.when(grp != order[-1])(far_relay)
    relay(order[-1])
    if far:
        pl.when(grp == order[-1])(far_relay)

    gt_mine = gt_out[...] + gt_half(0, last) if G > 1 else gt_half(0, last)
    rcopy(gt_send, gt_recv, s_pair.at[2], r_pair.at[2], sib).wait_recv()
    gt_out[...] = score_scale * (gt_mine + gt_recv[...])

    acc = partf[row]
    for j in near:
        acc = acc + taken(grp, j)
    gs_out[...] = acc
    for g in order:
        @pl.when(grp != g)
        def _(g=g):
            rcopy(zs.at[g], zr.at[g], s_zp.at[g], r_zp.at[g], sib).wait_recv()
            gs_out[...] = gs_out[...] + zr[g].astype(F32)
    if far:
        far_copy().wait_recv()
        gs_out[...] = score_scale * (gs_out[...] + dr[...].astype(F32))
    else:
        gs_out[...] = score_scale * gs_out[...]

    for c in sends:
        c.wait_send()
    if far:
        far_copy().wait_send()
    for g in range(G):
        lam_all(g).wait_send()
        for j in near:
            x_send(g, j).wait_send()
            p_send(g, j).wait_send()
        if far:
            d_send(g).wait_send()
            far_send(g).wait_send()

        @pl.when(grp != g)
        def _(g=g):
            z_send(g).wait_send()
            x_send(g, 0).wait_send()
            p_send(g, 0).wait_send()
            zp_send(g).wait_send()


def flush(gs, gt, gs_out, gt_out, sem):
    copies = [pltpu.make_async_copy(gt, gt_out, sem.at[0]), pltpu.make_async_copy(gs, gs_out, sem.at[1])]
    for c in copies:
        c.start()
    for c in copies:
        c.wait()


def per_device(R, NC, ND, source_desc, target_desc, target_dual, row_weight, matches):
    n, D = source_desc.shape
    own = target_desc.shape[0]
    G = (NC // 2) * ND
    C = R * n
    vm = pl.BlockSpec(memory_space=pltpu.VMEM)
    dma = pltpu.SemaphoreType.DMA
    outs = pl.pallas_call(
        functools.partial(kernel, R, NC, ND),
        out_shape=(jax.ShapeDtypeStruct((n, D), F32), jax.ShapeDtypeStruct((own, D), F32)),
        in_specs=[pl.BlockSpec(memory_space=pltpu.HBM)] * 5,
        out_specs=(vm, vm),
        scratch_shapes=[
            pltpu.VMEM((own, D), BF16),
            pltpu.VMEM((1, target_dual.shape[0]), F32),
            pltpu.VMEM((1, row_weight.shape[0]), F32),
            pltpu.VMEM((1, row_weight.shape[0]), jnp.int32),
            pltpu.VMEM((G, R, n, D), BF16),
            pltpu.VMEM((G, n, D), BF16),
            pltpu.VMEM((n, D), BF16),
            pltpu.VMEM((own, D), BF16),
            pltpu.VMEM((1, own), F32),
            pltpu.VMEM((1, own), F32),
            pltpu.VMEM((2, 2, G * n), F32),
            pltpu.VMEM((R, 2, G * n), F32),
            pltpu.VMEM((G, 2, C), F32),
            pltpu.VMEM((2 * own, 128), F32),
            pltpu.VMEM((G, 2 * own, C), F32),
            pltpu.VMEM((G, 1, C), F32),
            pltpu.VMEM((G, R * G, 1, C), F32),
            pltpu.VMEM((G, 2 * own, C), BF16),
            pltpu.VMEM((G, R, n, D), BF16),
            pltpu.VMEM((G, R, n, D), BF16),
            pltpu.VMEM((G, n, D), BF16),
            pltpu.VMEM((G, n, D), BF16),
            pltpu.VMEM((G, n, D), BF16),
            pltpu.VMEM((n, D), BF16),
            pltpu.VMEM((n, D), BF16),
            pltpu.VMEM((R, n, D), F32),
            pltpu.VMEM((own, D), F32),
            pltpu.VMEM((own, D), F32),
            dma((5,)),
            dma((3,)), dma((3,)),
            dma((G,)), dma((G,)),
            dma((R, G)), dma((R, G)),
            dma, dma,
            dma((G,)),
            dma((R,)), dma((R,)),
            dma((G,)), dma((G,)),
            dma((R, G)), dma((R, G)),
            dma((G,)), dma((G,)),
            dma((G,)), dma((G,)),
            dma, dma,
            pltpu.SemaphoreType.REGULAR,
        ],
        compiler_params=pltpu.CompilerParams(collective_id=0, has_side_effects=True,
                                             vmem_limit_bytes=32 * 1024 * 1024),
    )(*[pltpu.with_memory_space_constraint(a, pltpu.HBM) for a in (
        source_desc, target_desc, target_dual[None, :], row_weight[None, :], matches[None, :])])
    hbm = pl.BlockSpec(memory_space=pltpu.HBM)
    return pl.pallas_call(
        flush,
        out_shape=(jax.ShapeDtypeStruct((n, D), F32), jax.ShapeDtypeStruct((own, D), F32)),
        in_specs=[vm, vm],
        out_specs=(hbm, hbm),
        scratch_shapes=[dma((2,))],
        compiler_params=pltpu.CompilerParams(vmem_limit_bytes=8 * 1024 * 1024),
    )(*outs)


def solution(mesh):
    R, NC, ND = mesh.shape["row"], mesh.shape["col"], mesh.shape["depth"]
    return jax.shard_map(
        functools.partial(per_device, R, NC, ND),
        mesh=mesh,
        in_specs=(
            P(("row", "col", "depth"), None),
            P(("col", "depth", "row"), None),
            P(("col", "depth")),
            P("row"),
            P("row"),
        ),
        out_specs=(P(("row", "col", "depth"), None), P(("col", "depth", "row"), None)),
        check_vma=False,
    )
```

```python
import functools
import jax
import jax.numpy as jnp
from jax import lax
from jax.experimental import pallas as pl
from jax.experimental.pallas import tpu as pltpu
from jax.sharding import PartitionSpec as P

score_scale = 0.1875
F32 = jnp.float32
BF16 = jnp.bfloat16


def kernel(R, NC, ND, src_h, tgt_h, dual_h, weight_h, match_h, gs_out, gt_out,
           tgt, dual_all, weight, match_in, S, Q, QD, T2, dual, dual2, wm, wm_all, wm_g, dcol, e_buf, m_buf, lam,
           dbuf, ps, px, zs, zr, zd, ds, dr, partf, gt_send, gt_recv,
           s_in, s_pair, r_pair, s_z, r_z, s_x, r_x, s_qd, r_qd, s_d, s_wm, r_wm, s_l, r_l, s_p, r_p, s_zp, r_zp,
           s_zd, r_zd, s_dr, r_dr, line_in):
    G = (NC // 2) * ND
    N = R * G
    n, D = src_h.shape
    own = tgt_h.shape[0]
    C = R * n
    row = lax.axis_index("row")
    col = lax.axis_index("col")
    dep = lax.axis_index("depth")
    par = lax.rem(col, 2)
    grp = (col // 2) * ND + dep
    me = grp * R + row
    sib_col = col + 1 - 2 * par
    order = list(range(G))
    MESH = pl.DeviceIdType.MESH

    def flip(j):
        r, b = row, 1
        while b < R:
            if j & b:
                r = r + b * (1 - 2 * lax.rem(row // b, 2))
            b *= 2
        return r

    if R & (R - 1) == 0:
        rows = [flip(j) for j in range(R)]
    else:
        rows = [lax.rem(row + j, R) for j in range(R)]
    far = R >= 4 and R & (R - 1) == 0
    near = range(1, R - 1) if far else range(1, R)
    rd = rows[R - 1]

    def dev(r, c, d):
        return {"row": r, "col": c, "depth": d}

    sib = dev(row, sib_col, dep)

    def zdev(g):
        return dev(row, (g // ND) * 2 + par, g % ND)

    def zrel(g):
        return dev(row, (g // ND) * 2 + 1 - par, g % ND)

    def xdev(j):
        return dev(rows[j], col, dep)

    def xrel(j):
        return dev(rows[j], sib_col, dep)

    def peer(k):
        i = lax.rem(me + k, N)
        g = i // R
        return dev(lax.rem(i, R), (g // ND) * 2 + par, lax.rem(g, ND))

    def rcopy(a, b, ss, rs, to):
        return pltpu.make_async_remote_copy(src_ref=a, dst_ref=b, send_sem=ss, recv_sem=rs,
                                            device_id=to, device_id_type=MESH)

    def each_peer(fn):
        if N <= 32:
            for g in range(G):
                for j in range(R - 1, 0, -1):
                    fn(dev(rows[j], (g // ND) * 2 + par, g % ND))

                @pl.when(grp != g)
                def _(g=g):
                    fn(zdev(g))
        else:
            lax.fori_loop(1, N, lambda k, c: (fn(peer(k)), c)[1], 0)

    def greet(sem, to):
        pl.semaphore_signal(sem, inc=1, device_id=to, device_id_type=MESH)

    barrier = pltpu.get_barrier_semaphore()
    for g in range(G):
        @pl.when(grp != g)
        def _(g=g):
            greet(barrier, zrel(g))
    for j in near:
        greet(barrier, xdev(j))
        greet(barrier, xrel(j))
    if far:
        greet(barrier, xrel(R - 1))
    greet(barrier, sib)
    loads = [pltpu.make_async_copy(a, b, s_in.at[i]) for i, (a, b) in enumerate((
        (src_h, S.at[grp, row]), (tgt_h, tgt), (dual_h, dual_all), (weight_h, weight), (match_h, match_in)))]
    for c in loads:
        c.start()
    pl.semaphore_wait(barrier, G + 2 * len(near) + (1 if far else 0))

    sends = []

    def go(c):
        c.start()
        sends.append(c)

    mine = src_h

    def z_send(g):
        return rcopy(mine, Q.at[grp], s_z.at[g], r_z.at[grp], zrel(g))

    tour = [jnp.where(grp == 0, G - 1 - k, k) for k in range(G)]
    for g in tour:
        @pl.when(grp != g)
        def _(g=g):
            z_send(g).start()
    if far:
        go(rcopy(mine, QD, s_qd, r_qd, xrel(R - 1)))
    for j in near:
        rcopy(mine, S.at[grp, row], s_x.at[j, grp], r_x.at[row, grp], xdev(j)).start()
    go(rcopy(tgt_h, T2, s_pair.at[0], r_pair.at[0], sib))
    for j in range(1, R):
        greet(line_in, xrel(j))
    greet(line_in, sib)
    for c in loads[2:]:
        c.wait()
    dual[...] = dual_all[:, pl.ds(pl.multiple_of(row * own, own), own)]
    go(rcopy(dual, dual2, s_pair.at[1], r_pair.at[1], sib))

    for i, vec in ((0, weight[...]), (1, match_in[...].astype(F32))):
        span = ND * n
        for q in range(2):
            parts = [jnp.where(par == q, vec[:, 2 * c * span:(2 * c + 1) * span],
                               vec[:, (2 * c + 1) * span:(2 * c + 2) * span]) for c in range(NC // 2)]
            wm[q, i:i + 1, :] = parts[0] if len(parts) == 1 else jnp.concatenate(parts, axis=1)
    wm_all[row] = wm[0]
    for j in range(1, R):
        go(rcopy(wm.at[1], wm_all.at[row], s_wm.at[j], r_wm.at[row], xrel(j)))

    def x_send(g, j):
        return rcopy(Q.at[g], S.at[g, row], s_x.at[j, g], r_x.at[row, g], sib if j == 0 else xrel(j))

    def d_send(g):
        return rcopy(QD, S.at[grp, rd], s_d.at[g], r_x.at[rd, grp], zrel(g))

    hops = [0] + list(near)
    if far:
        rcopy(QD, QD, s_qd, r_qd, xrel(R - 1)).wait_recv()
        for g in tour:
            d_send(g).start()
    for g in order:
        @pl.when(grp != g)
        def _(g=g):
            rcopy(Q.at[g], Q.at[g], s_z.at[g], r_z.at[g], zrel(g)).wait_recv()
            for j in list(near) + [0]:
                x_send(g, j).start()
    dcol[0:own, :] = jnp.transpose(jnp.broadcast_to(dual[...], (128, own)))
    for c in loads[:2]:
        c.wait()
    rcopy(dual, dual2, s_pair.at[1], r_pair.at[1], sib).wait_recv()
    dcol[own:2 * own, :] = jnp.transpose(jnp.broadcast_to(dual2[...], (128, own)))
    rcopy(tgt, T2, s_pair.at[0], r_pair.at[0], sib).wait_recv()

    lane_rep = C // 128

    def scores_chunk(g):
        block = S[g].reshape(C, D)
        tops = []
        for h, t in ((0, tgt), (1, T2)):
            p = lax.dot_general(t[...], block, (((1,), (1,)), ((), ())), preferred_element_type=F32)
            dc = dcol[h * own:(h + 1) * own, :]
            s = score_scale * p + jnp.concatenate([dc] * lane_rep, axis=1)
            e_buf[g, h * own:(h + 1) * own, :] = s
            tops.append(jnp.max(s, axis=0, keepdims=True))
        top = jnp.maximum(tops[0], tops[1])
        m_buf[g] = top
        e = jnp.exp(e_buf[g] - top)
        e_buf[g] = e
        lam[g, me] = top + jnp.log(jnp.sum(e, axis=0, keepdims=True))

    def take(g, r):
        rcopy(S.at[g, r], S.at[g, r], s_x.at[0, 0], r_x.at[r, g], sib).wait_recv()

    place = sum(i * (grp == g).astype(jnp.int32) for i, g in enumerate(order))
    for i in range(G):
        g = grp if i == 0 else jnp.where(place >= i, order[i - 1], order[i])
        for j in range(0 if i else 1, R):
            take(g, rows[j])
        scores_chunk(g)
        if i == 0:
            pl.semaphore_wait(line_in, R)
        each_peer(lambda to: rcopy(lam.at[g, me], lam.at[g, me], s_l.at[g], r_l.at[g], to).start())

    for j in range(1, R):
        rcopy(wm.at[1], wm_all.at[rows[j]], s_wm.at[j], r_wm.at[rows[j]], xrel(j)).wait_recv()
    for g in range(G):
        for i in range(2):
            wm_g[g, i:i + 1, :] = jnp.concatenate(
                [wm_all[r, i:i + 1, g * n:(g + 1) * n] for r in range(R)], axis=1)

    first = [((c * ND + dep) * R + row) * own for c in (col, sib_col)]

    def lam_all(g):
        every = lam.at[g, pl.ds(0, N - 1)]
        return rcopy(every, every, s_l.at[g], r_l.at[g], sib)

    def delta_chunk(g):
        lam_all(g).wait_recv()
        parts = lam[g]
        peak = jnp.max(parts, axis=0)
        log_total = peak + jnp.log(jnp.sum(jnp.exp(parts - peak[None]), axis=0))
        w = wm_g[g, 0:1, :]
        match = wm_g[g, 1:2, :].astype(jnp.int32)
        scale = w * jnp.exp(m_buf[g] - log_total)
        part = None
        for h, t in ((0, tgt), (1, T2)):
            ids = lax.broadcasted_iota(jnp.int32, (own, C), 0)
            hit = jnp.where(ids == match - first[h], w, 0.0)
            d = (scale * e_buf[g, h * own:(h + 1) * own, :] - hit).astype(BF16)
            dbuf[g, h * own:(h + 1) * own, :] = d
            q = lax.dot_general(d, t[...], (((0,), (0,)), ((), ())), preferred_element_type=F32)
            part = q if part is None else part + q
        return part

    def p_send(g, j):
        apart = (grp != g).astype(jnp.int32)
        to = sib if j == 0 else dev(rows[j], col + apart * (sib_col - col), dep)
        return rcopy(ps.at[g, rows[j]], px.at[g, row], s_p.at[j, g], r_p.at[row, g], to)

    def far_send(g):
        return rcopy(ps.at[g, rd], zd.at[grp], s_zd.at[g], r_zd.at[grp], zrel(g))

    def gt_half(h, groups):
        acc = None
        for g in groups:
            q = jnp.dot(dbuf[g, h * own:(h + 1) * own, :], S[g].reshape(C, D), preferred_element_type=F32)
            acc = q if acc is None else acc + q
        return acc

    for i, g in enumerate(order):
        if i == G - 1 and G > 1:
            gt_send[...] = gt_half(1, order[:-1])
            gt_out[...] = gt_half(0, order[:-1])
        part = delta_chunk(g).reshape(R, n, D)
        ps[g] = part.astype(BF16)
        if far:
            far_send(g).start()
        for j in near:
            p_send(g, j).start()

        @pl.when(grp != g)
        def _(g=g):
            p_send(g, 0).start()

        @pl.when(grp == g)
        def _(part=part):
            partf[...] = part

    last = order[-1:]
    gt_send[...] = gt_send[...] + gt_half(1, last) if G > 1 else gt_half(1, last)
    go(rcopy(gt_send, gt_recv, s_pair.at[2], r_pair.at[2], sib))

    def taken(g, j):
        rcopy(ps.at[g, rows[j]], px.at[g, rows[j]], s_p.at[j, g], r_p.at[rows[j], g], sib).wait_recv()
        return px[g, rows[j]].astype(F32)

    def zp_send(g):
        return rcopy(zs.at[g], zr.at[grp], s_zp.at[g], r_zp.at[grp], zrel(g))

    def relay(g):
        @pl.when(grp != g)
        def _():
            acc = taken(g, 0)
            for j in near:
                acc = acc + taken(g, j)
            zs[g] = acc.astype(BF16)
            zp_send(g).start()

    def far_copy():
        return rcopy(ds, dr, s_dr, r_dr, xrel(R - 1))

    def far_relay():
        acc = None
        for g in range(G):
            rcopy(zs.at[g], zd.at[g], s_zd.at[g], r_zd.at[g], sib).wait_recv()
            acc = zd[g].astype(F32) if acc is None else acc + zd[g].astype(F32)
        ds[...] = acc.astype(BF16)
        far_copy().start()

    for g in order[:-1]:
        relay(g)
    if far:
        pl.when(grp != order[-1])(far_relay)
    relay(order[-1])
    if far:
        pl.when(grp == order[-1])(far_relay)

    gt_mine = gt_out[...] + gt_half(0, last) if G > 1 else gt_half(0, last)
    rcopy(gt_send, gt_recv, s_pair.at[2], r_pair.at[2], sib).wait_recv()
    gt_out[...] = score_scale * (gt_mine + gt_recv[...])

    acc = partf[row]
    for j in near:
        acc = acc + taken(grp, j)
    gs_out[...] = acc
    for g in order:
        @pl.when(grp != g)
        def _(g=g):
            rcopy(zs.at[g], zr.at[g], s_zp.at[g], r_zp.at[g], sib).wait_recv()
            gs_out[...] = gs_out[...] + zr[g].astype(F32)
    if far:
        far_copy().wait_recv()
        gs_out[...] = score_scale * (gs_out[...] + dr[...].astype(F32))
    else:
        gs_out[...] = score_scale * gs_out[...]

    for c in sends:
        c.wait_send()
    if far:
        far_copy().wait_send()
    for g in range(G):
        lam_all(g).wait_send()
        for j in near:
            x_send(g, j).wait_send()
            p_send(g, j).wait_send()
        if far:
            d_send(g).wait_send()
            far_send(g).wait_send()

        @pl.when(grp != g)
        def _(g=g):
            z_send(g).wait_send()
            x_send(g, 0).wait_send()
            p_send(g, 0).wait_send()
            zp_send(g).wait_send()


def flush(gs, gt, gs_out, gt_out, sem):
    copies = [pltpu.make_async_copy(gt, gt_out, sem.at[0]), pltpu.make_async_copy(gs, gs_out, sem.at[1])]
    for c in copies:
        c.start()
    for c in copies:
        c.wait()


def per_device(R, NC, ND, source_desc, target_desc, target_dual, row_weight, matches):
    n, D = source_desc.shape
    own = target_desc.shape[0]
    G = (NC // 2) * ND
    C = R * n
    vm = pl.BlockSpec(memory_space=pltpu.VMEM)
    dma = pltpu.SemaphoreType.DMA
    outs = pl.pallas_call(
        functools.partial(kernel, R, NC, ND),
        out_shape=(jax.ShapeDtypeStruct((n, D), F32), jax.ShapeDtypeStruct((own, D), F32)),
        in_specs=[pl.BlockSpec(memory_space=pltpu.HBM)] * 5,
        out_specs=(vm, vm),
        scratch_shapes=[
            pltpu.VMEM((own, D), BF16),
            pltpu.VMEM((1, target_dual.shape[0]), F32),
            pltpu.VMEM((1, row_weight.shape[0]), F32),
            pltpu.VMEM((1, row_weight.shape[0]), jnp.int32),
            pltpu.VMEM((G, R, n, D), BF16),
            pltpu.VMEM((G, n, D), BF16),
            pltpu.VMEM((n, D), BF16),
            pltpu.VMEM((own, D), BF16),
            pltpu.VMEM((1, own), F32),
            pltpu.VMEM((1, own), F32),
            pltpu.VMEM((2, 2, G * n), F32),
            pltpu.VMEM((R, 2, G * n), F32),
            pltpu.VMEM((G, 2, C), F32),
            pltpu.VMEM((2 * own, 128), F32),
            pltpu.VMEM((G, 2 * own, C), F32),
            pltpu.VMEM((G, 1, C), F32),
            pltpu.VMEM((G, R * G, 1, C), F32),
            pltpu.VMEM((G, 2 * own, C), BF16),
            pltpu.VMEM((G, R, n, D), BF16),
            pltpu.VMEM((G, R, n, D), BF16),
            pltpu.VMEM((G, n, D), BF16),
            pltpu.VMEM((G, n, D), BF16),
            pltpu.VMEM((G, n, D), BF16),
            pltpu.VMEM((n, D), BF16),
            pltpu.VMEM((n, D), BF16),
            pltpu.VMEM((R, n, D), F32),
            pltpu.VMEM((own, D), F32),
            pltpu.VMEM((own, D), F32),
            dma((5,)),
            dma((3,)), dma((3,)),
            dma((G,)), dma((G,)),
            dma((R, G)), dma((R, G)),
            dma, dma,
            dma((G,)),
            dma((R,)), dma((R,)),
            dma((G,)), dma((G,)),
            dma((R, G)), dma((R, G)),
            dma((G,)), dma((G,)),
            dma((G,)), dma((G,)),
            dma, dma,
            pltpu.SemaphoreType.REGULAR,
        ],
        compiler_params=pltpu.CompilerParams(collective_id=0, has_side_effects=True,
                                             vmem_limit_bytes=32 * 1024 * 1024),
    )(*[pltpu.with_memory_space_constraint(a, pltpu.HBM) for a in (
        source_desc, target_desc, target_dual[None, :], row_weight[None, :], matches[None, :])])
    hbm = pl.BlockSpec(memory_space=pltpu.HBM)
    return pl.pallas_call(
        flush,
        out_shape=(jax.ShapeDtypeStruct((n, D), F32), jax.ShapeDtypeStruct((own, D), F32)),
        in_specs=[vm, vm],
        out_specs=(hbm, hbm),
        scratch_shapes=[dma((2,))],
        compiler_params=pltpu.CompilerParams(vmem_limit_bytes=8 * 1024 * 1024),
    )(*outs)


def solution(mesh):
    R, NC, ND = mesh.shape["row"], mesh.shape["col"], mesh.shape["depth"]
    return jax.shard_map(
        functools.partial(per_device, R, NC, ND),
        mesh=mesh,
        in_specs=(
            P(("row", "col", "depth"), None),
            P(("col", "depth", "row"), None),
            P(("col", "depth")),
            P("row"),
            P("row"),
        ),
        out_specs=(P(("row", "col", "depth"), None), P(("col", "depth", "row"), None)),
        check_vma=False,
    )
```

```python
import functools
import jax
import jax.numpy as jnp
from jax import lax
from jax.experimental import pallas as pl
from jax.experimental.pallas import tpu as pltpu
from jax.sharding import PartitionSpec as P

score_scale = 0.1875
F32 = jnp.float32
BF16 = jnp.bfloat16


def kernel(R, NC, ND, src_h, tgt_h, dual_h, weight_h, match_h, gs_out, gt_out,
           tgt, dual_all, weight, match_in, S, Q, QD, T2, dual, dual2, wm, wm_all, wm_g, dcol, e_buf, m_buf, lam,
           dbuf, U, H, em, ps, px, zs, zr, zd, ds, dr, partf, gt_send, gt_recv,
           s_in, s_pair, r_pair, s_z, r_z, s_x, r_x, s_qd, r_qd, s_d, s_wm, r_wm, s_l, r_l, s_p, r_p, s_zp, r_zp,
           s_zd, r_zd, s_dr, r_dr, line_in):
    G = (NC // 2) * ND
    N = R * G
    n, D = src_h.shape
    own = tgt_h.shape[0]
    C = R * n
    row = lax.axis_index("row")
    col = lax.axis_index("col")
    dep = lax.axis_index("depth")
    par = lax.rem(col, 2)
    grp = (col // 2) * ND + dep
    me = grp * R + row
    sib_col = col + 1 - 2 * par
    order = list(range(G))
    MESH = pl.DeviceIdType.MESH

    def flip(j):
        r, b = row, 1
        while b < R:
            if j & b:
                r = r + b * (1 - 2 * lax.rem(row // b, 2))
            b *= 2
        return r

    if R & (R - 1) == 0:
        rows = [flip(j) for j in range(R)]
    else:
        rows = [lax.rem(row + j, R) for j in range(R)]
    far = R >= 4 and R & (R - 1) == 0
    near = range(1, R - 1) if far else range(1, R)
    rd = rows[R - 1]

    def dev(r, c, d):
        return {"row": r, "col": c, "depth": d}

    sib = dev(row, sib_col, dep)

    def zdev(g):
        return dev(row, (g // ND) * 2 + par, g % ND)

    def zrel(g):
        return dev(row, (g // ND) * 2 + 1 - par, g % ND)

    def xdev(j):
        return dev(rows[j], col, dep)

    def xrel(j):
        return dev(rows[j], sib_col, dep)

    def peer(k):
        i = lax.rem(me + k, N)
        g = i // R
        return dev(lax.rem(i, R), (g // ND) * 2 + par, lax.rem(g, ND))

    def rcopy(a, b, ss, rs, to):
        return pltpu.make_async_remote_copy(src_ref=a, dst_ref=b, send_sem=ss, recv_sem=rs,
                                            device_id=to, device_id_type=MESH)

    def each_peer(fn):
        if N <= 32:
            for g in range(G):
                for j in range(R - 1, 0, -1):
                    fn(dev(rows[j], (g // ND) * 2 + par, g % ND))

                @pl.when(grp != g)
                def _(g=g):
                    fn(zdev(g))
        else:
            lax.fori_loop(1, N, lambda k, c: (fn(peer(k)), c)[1], 0)

    def greet(sem, to):
        pl.semaphore_signal(sem, inc=1, device_id=to, device_id_type=MESH)

    barrier = pltpu.get_barrier_semaphore()
    for g in range(G):
        @pl.when(grp != g)
        def _(g=g):
            greet(barrier, zrel(g))
    for j in near:
        greet(barrier, xdev(j))
        greet(barrier, xrel(j))
    if far:
        greet(barrier, xrel(R - 1))
    greet(barrier, sib)
    loads = [pltpu.make_async_copy(a, b, s_in.at[i]) for i, (a, b) in enumerate((
        (src_h, S.at[grp, row]), (tgt_h, tgt), (dual_h, dual_all), (weight_h, weight), (match_h, match_in)))]
    for c in loads:
        c.start()
    for c in loads[:2]:
        c.wait()
    pl.semaphore_wait(barrier, G + 2 * len(near) + (1 if far else 0))

    sends = []

    def go(c):
        c.start()
        sends.append(c)

    mine = S.at[grp, row]

    def z_send(g):
        return rcopy(mine, Q.at[grp], s_z.at[g], r_z.at[grp], zrel(g))

    tour = [jnp.where(grp == 0, G - 1 - k, k) for k in range(G)]
    for g in tour:
        @pl.when(grp != g)
        def _(g=g):
            z_send(g).start()
    if far:
        go(rcopy(mine, QD, s_qd, r_qd, xrel(R - 1)))
    for j in near:
        rcopy(mine, S.at[grp, row], s_x.at[j, grp], r_x.at[row, grp], xdev(j)).start()
    go(rcopy(tgt, T2, s_pair.at[0], r_pair.at[0], sib))
    for j in range(1, R):
        greet(line_in, xrel(j))
    greet(line_in, sib)
    for c in loads[2:]:
        c.wait()
    dual[...] = dual_all[:, pl.ds(pl.multiple_of(row * own, own), own)]
    go(rcopy(dual, dual2, s_pair.at[1], r_pair.at[1], sib))

    for i, vec in ((0, weight[...]), (1, match_in[...].astype(F32))):
        span = ND * n
        for q in range(2):
            parts = [jnp.where(par == q, vec[:, 2 * c * span:(2 * c + 1) * span],
                               vec[:, (2 * c + 1) * span:(2 * c + 2) * span]) for c in range(NC // 2)]
            wm[q, i:i + 1, :] = parts[0] if len(parts) == 1 else jnp.concatenate(parts, axis=1)
    wm_all[row] = wm[0]
    for j in range(1, R):
        go(rcopy(wm.at[1], wm_all.at[row], s_wm.at[j], r_wm.at[row], xrel(j)))

    def x_send(g, j):
        return rcopy(Q.at[g], S.at[g, row], s_x.at[j, g], r_x.at[row, g], sib if j == 0 else xrel(j))

    def d_send(g):
        return rcopy(QD, S.at[grp, rd], s_d.at[g], r_x.at[rd, grp], zrel(g))

    hops = [0] + list(near)
    if far:
        rcopy(QD, QD, s_qd, r_qd, xrel(R - 1)).wait_recv()
        for g in tour:
            d_send(g).start()
    for g in order:
        @pl.when(grp != g)
        def _(g=g):
            rcopy(Q.at[g], Q.at[g], s_z.at[g], r_z.at[g], zrel(g)).wait_recv()
            for j in list(near) + [0]:
                x_send(g, j).start()
    dcol[0:own, :] = jnp.transpose(jnp.broadcast_to(dual[...], (128, own)))
    rcopy(dual, dual2, s_pair.at[1], r_pair.at[1], sib).wait_recv()
    dcol[own:2 * own, :] = jnp.transpose(jnp.broadcast_to(dual2[...], (128, own)))
    rcopy(tgt, T2, s_pair.at[0], r_pair.at[0], sib).wait_recv()

    lane_rep = C // 128

    def scores_chunk(g):
        block = S[g].reshape(C, D)
        tops = []
        for h, t in ((0, tgt), (1, T2)):
            p = lax.dot_general(t[...], block, (((1,), (1,)), ((), ())), preferred_element_type=F32)
            dc = dcol[h * own:(h + 1) * own, :]
            s = score_scale * p + jnp.concatenate([dc] * lane_rep, axis=1)
            e_buf[g, h * own:(h + 1) * own, :] = s
            tops.append(jnp.max(s, axis=0, keepdims=True))
        top = jnp.maximum(tops[0], tops[1])
        m_buf[g] = top
        e = jnp.exp(e_buf[g] - top)
        e_buf[g] = e
        lam[g, me] = top + jnp.log(jnp.sum(e, axis=0, keepdims=True))

    def take(g, r):
        rcopy(S.at[g, r], S.at[g, r], s_x.at[0, 0], r_x.at[r, g], sib).wait_recv()

    place = sum(i * (grp == g).astype(jnp.int32) for i, g in enumerate(order))
    for i in range(G):
        g = grp if i == 0 else jnp.where(place >= i, order[i - 1], order[i])
        for j in range(0 if i else 1, R):
            take(g, rows[j])
        scores_chunk(g)
        if i == 0:
            pl.semaphore_wait(line_in, R)
        each_peer(lambda to: rcopy(lam.at[g, me], lam.at[g, me], s_l.at[g], r_l.at[g], to).start())

    for j in range(1, R):
        rcopy(wm.at[1], wm_all.at[rows[j]], s_wm.at[j], r_wm.at[rows[j]], xrel(j)).wait_recv()
    for g in range(G):
        for i in range(2):
            wm_g[g, i:i + 1, :] = jnp.concatenate(
                [wm_all[r, i:i + 1, g * n:(g + 1) * n] for r in range(R)], axis=1)

    first = [((c * ND + dep) * R + row) * own for c in (col, sib_col)]

    def lam_all(g):
        every = lam.at[g, pl.ds(0, N - 1)]
        return rcopy(every, every, s_l.at[g], r_l.at[g], sib)

    halves = ((0, tgt), (1, T2))
    over_targets = (((0,), (0,)), ((), ()))

    def hits(g, h):
        match = wm_g[g, 1:2, :].astype(jnp.int32)
        return lax.broadcasted_iota(jnp.int32, (own, C), 0) == match - first[h]

    def scale_of(g):
        lam_all(g).wait_recv()
        parts = lam[g]
        peak = jnp.max(parts, axis=0)
        log_total = peak + jnp.log(jnp.sum(jnp.exp(parts - peak[None]), axis=0))
        return wm_g[g, 0:1, :] * jnp.exp(m_buf[g] - log_total)

    def round_delta(g, h, scale):
        hit = jnp.where(hits(g, h), wm_g[g, 0:1, :], 0.0)
        d = (scale * e_buf[g, h * own:(h + 1) * own, :] - hit).astype(BF16)
        dbuf[g, h * own:(h + 1) * own, :] = d
        return d

    def delta_chunk(g):
        scale = scale_of(g)
        part = None
        for h, t in halves:
            q = lax.dot_general(round_delta(g, h, scale), t[...], over_targets, preferred_element_type=F32)
            part = q if part is None else part + q
        return part

    def prepare(g):
        u = k = m = None
        for h, t in halves:
            e = e_buf[g, h * own:(h + 1) * own, :]
            hit = hits(g, h)
            at = jnp.sum(jnp.where(hit, e, 0.0), axis=0, keepdims=True)
            uh = lax.dot_general(jnp.where(hit, 0.0, e).astype(BF16), t[...], over_targets, preferred_element_type=F32)
            kh = lax.dot_general(jnp.where(hit, 1.0, 0.0).astype(BF16), t[...], over_targets, preferred_element_type=F32)
            u, k, m = (uh, kh, at) if h == 0 else (u + uh, k + kh, m + at)
        U[...] = u
        H[...] = k
        em[...] = m

    def prepared(g):
        scale = scale_of(g)
        m_buf[g] = scale
        coef = (scale * em[...] - wm_g[g, 0:1, :]).astype(BF16).astype(F32)

        def down(v):
            return jnp.concatenate([jnp.transpose(jnp.broadcast_to(v, (128, C)))] * (D // 128), axis=1)

        return down(scale) * U[...] + down(coef) * H[...]

    def p_send(g, j):
        apart = (grp != g).astype(jnp.int32)
        to = sib if j == 0 else dev(rows[j], col + apart * (sib_col - col), dep)
        return rcopy(ps.at[g, rows[j]], px.at[g, row], s_p.at[j, g], r_p.at[row, g], to)

    def far_send(g):
        return rcopy(ps.at[g, rd], zd.at[grp], s_zd.at[g], r_zd.at[grp], zrel(g))

    def gt_half(h, groups):
        acc = None
        for g in groups:
            q = jnp.dot(dbuf[g, h * own:(h + 1) * own, :], S[g].reshape(C, D), preferred_element_type=F32)
            acc = q if acc is None else acc + q
        return acc

    prepare(order[0])

    def taken(g, j):
        rcopy(ps.at[g, rows[j]], px.at[g, rows[j]], s_p.at[j, g], r_p.at[rows[j], g], sib).wait_recv()
        return px[g, rows[j]].astype(F32)

    def zp_send(g):
        return rcopy(zs.at[g], zr.at[grp], s_zp.at[g], r_zp.at[grp], zrel(g))

    def relay(g):
        @pl.when(grp != g)
        def _():
            acc = taken(g, 0)
            for j in near:
                acc = acc + taken(g, j)
            zs[g] = acc.astype(BF16)
            zp_send(g).start()

    for i, g in enumerate(order):
        if i == G - 1 and G > 1:
            gt_send[...] = gt_half(1, order[:-1])
        part = (prepared(g) if i == 0 else delta_chunk(g)).reshape(R, n, D)
        ps[g] = part.astype(BF16)
        if far:
            far_send(g).start()
        for j in near:
            p_send(g, j).start()

        @pl.when(grp != g)
        def _(g=g):
            p_send(g, 0).start()

        @pl.when(grp == g)
        def _(part=part):
            partf[...] = part

        if i == 0:
            for h in range(2):
                round_delta(g, h, m_buf[g])

    last = order[-1:]
    gt_send[...] = gt_send[...] + gt_half(1, last) if G > 1 else gt_half(1, last)
    go(rcopy(gt_send, gt_recv, s_pair.at[2], r_pair.at[2], sib))

    def far_copy():
        return rcopy(ds, dr, s_dr, r_dr, xrel(R - 1))

    def far_relay():
        acc = None
        for g in range(G):
            rcopy(zs.at[g], zd.at[g], s_zd.at[g], r_zd.at[g], sib).wait_recv()
            acc = zd[g].astype(F32) if acc is None else acc + zd[g].astype(F32)
        ds[...] = acc.astype(BF16)
        far_copy().start()

    for i, g in enumerate(order):
        relay(g)
        if far:
            pl.when(grp == g)(far_relay)

    gt_mine = gt_half(0, order)
    rcopy(gt_send, gt_recv, s_pair.at[2], r_pair.at[2], sib).wait_recv()
    gt_out[...] = score_scale * (gt_mine + gt_recv[...])

    acc = partf[row]
    for j in near:
        acc = acc + taken(grp, j)
    gs_out[...] = acc
    for g in order:
        @pl.when(grp != g)
        def _(g=g):
            rcopy(zs.at[g], zr.at[g], s_zp.at[g], r_zp.at[g], sib).wait_recv()
            gs_out[...] = gs_out[...] + zr[g].astype(F32)
    if far:
        far_copy().wait_recv()
        gs_out[...] = score_scale * (gs_out[...] + dr[...].astype(F32))
    else:
        gs_out[...] = score_scale * gs_out[...]

    for c in sends:
        c.wait_send()
    if far:
        far_copy().wait_send()
    for g in range(G):
        lam_all(g).wait_send()
        for j in near:
            x_send(g, j).wait_send()
            p_send(g, j).wait_send()
        if far:
            d_send(g).wait_send()
            far_send(g).wait_send()

        @pl.when(grp != g)
        def _(g=g):
            z_send(g).wait_send()
            x_send(g, 0).wait_send()
            p_send(g, 0).wait_send()
            zp_send(g).wait_send()


def flush(gs, gt, gs_out, gt_out, sem):
    copies = [pltpu.make_async_copy(gt, gt_out, sem.at[0]), pltpu.make_async_copy(gs, gs_out, sem.at[1])]
    for c in copies:
        c.start()
    for c in copies:
        c.wait()


def per_device(R, NC, ND, source_desc, target_desc, target_dual, row_weight, matches):
    n, D = source_desc.shape
    own = target_desc.shape[0]
    G = (NC // 2) * ND
    C = R * n
    vm = pl.BlockSpec(memory_space=pltpu.VMEM)
    dma = pltpu.SemaphoreType.DMA
    outs = pl.pallas_call(
        functools.partial(kernel, R, NC, ND),
        out_shape=(jax.ShapeDtypeStruct((n, D), F32), jax.ShapeDtypeStruct((own, D), F32)),
        in_specs=[pl.BlockSpec(memory_space=pltpu.HBM)] * 5,
        out_specs=(vm, vm),
        scratch_shapes=[
            pltpu.VMEM((own, D), BF16),
            pltpu.VMEM((1, target_dual.shape[0]), F32),
            pltpu.VMEM((1, row_weight.shape[0]), F32),
            pltpu.VMEM((1, row_weight.shape[0]), jnp.int32),
            pltpu.VMEM((G, R, n, D), BF16),
            pltpu.VMEM((G, n, D), BF16),
            pltpu.VMEM((n, D), BF16),
            pltpu.VMEM((own, D), BF16),
            pltpu.VMEM((1, own), F32),
            pltpu.VMEM((1, own), F32),
            pltpu.VMEM((2, 2, G * n), F32),
            pltpu.VMEM((R, 2, G * n), F32),
            pltpu.VMEM((G, 2, C), F32),
            pltpu.VMEM((2 * own, 128), F32),
            pltpu.VMEM((G, 2 * own, C), F32),
            pltpu.VMEM((G, 1, C), F32),
            pltpu.VMEM((G, R * G, 1, C), F32),
            pltpu.VMEM((G, 2 * own, C), BF16),
            pltpu.VMEM((C, D), F32),
            pltpu.VMEM((C, D), F32),
            pltpu.VMEM((1, C), F32),
            pltpu.VMEM((G, R, n, D), BF16),
            pltpu.VMEM((G, R, n, D), BF16),
            pltpu.VMEM((G, n, D), BF16),
            pltpu.VMEM((G, n, D), BF16),
            pltpu.VMEM((G, n, D), BF16),
            pltpu.VMEM((n, D), BF16),
            pltpu.VMEM((n, D), BF16),
            pltpu.VMEM((R, n, D), F32),
            pltpu.VMEM((own, D), F32),
            pltpu.VMEM((own, D), F32),
            dma((5,)),
            dma((3,)), dma((3,)),
            dma((G,)), dma((G,)),
            dma((R, G)), dma((R, G)),
            dma, dma,
            dma((G,)),
            dma((R,)), dma((R,)),
            dma((G,)), dma((G,)),
            dma((R, G)), dma((R, G)),
            dma((G,)), dma((G,)),
            dma((G,)), dma((G,)),
            dma, dma,
            pltpu.SemaphoreType.REGULAR,
        ],
        compiler_params=pltpu.CompilerParams(collective_id=0, has_side_effects=True,
                                             vmem_limit_bytes=32 * 1024 * 1024),
    )(*[pltpu.with_memory_space_constraint(a, pltpu.HBM) for a in (
        source_desc, target_desc, target_dual[None, :], row_weight[None, :], matches[None, :])])
    hbm = pl.BlockSpec(memory_space=pltpu.HBM)
    return pl.pallas_call(
        flush,
        out_shape=(jax.ShapeDtypeStruct((n, D), F32), jax.ShapeDtypeStruct((own, D), F32)),
        in_specs=[vm, vm],
        out_specs=(hbm, hbm),
        scratch_shapes=[dma((2,))],
        compiler_params=pltpu.CompilerParams(vmem_limit_bytes=8 * 1024 * 1024),
    )(*outs)


def solution(mesh):
    R, NC, ND = mesh.shape["row"], mesh.shape["col"], mesh.shape["depth"]
    return jax.shard_map(
        functools.partial(per_device, R, NC, ND),
        mesh=mesh,
        in_specs=(
            P(("row", "col", "depth"), None),
            P(("col", "depth", "row"), None),
            P(("col", "depth")),
            P("row"),
            P("row"),
        ),
        out_specs=(P(("row", "col", "depth"), None), P(("col", "depth", "row"), None)),
        check_vma=False,
    )
```

```python
import functools
import jax
import jax.numpy as jnp
from jax import lax
from jax.experimental import pallas as pl
from jax.experimental.pallas import tpu as pltpu
from jax.sharding import PartitionSpec as P

score_scale = 0.1875
log2e = 1.4426950408889634
F32 = jnp.float32
BF16 = jnp.bfloat16


def kernel(R, NC, ND, src_h, tgt_h, dual_h, weight_h, match_h, gs_out, gt_out,
           tgt, dual_all, weight, match_in, S, Q, QD, T2, dual, dual2, wm, wm_all, wm_g, dcol, e_buf, m_buf, lam,
           dbuf, U, H, em, ps, px, zs, zr, zd, ds, dr, partf, gt_send, gt_recv,
           s_in, s_pair, r_pair, s_z, r_z, s_x, r_x, s_qd, r_qd, s_d, s_wm, r_wm, s_l, r_l, s_p, r_p, s_zp, r_zp,
           s_zd, r_zd, s_dr, r_dr, line_in):
    G = (NC // 2) * ND
    N = R * G
    n, D = src_h.shape
    own = tgt_h.shape[0]
    C = R * n
    row = lax.axis_index("row")
    col = lax.axis_index("col")
    dep = lax.axis_index("depth")
    par = lax.rem(col, 2)
    grp = (col // 2) * ND + dep
    me = grp * R + row
    sib_col = col + 1 - 2 * par
    order = sorted(range(G), key=lambda g: (g > 0) - (g == G - 1))
    MESH = pl.DeviceIdType.MESH

    def flip(j):
        r, b = row, 1
        while b < R:
            if j & b:
                r = r + b * (1 - 2 * lax.rem(row // b, 2))
            b *= 2
        return r

    if R & (R - 1) == 0:
        rows = [flip(j) for j in range(R)]
    else:
        rows = [lax.rem(row + j, R) for j in range(R)]
    far = R >= 4 and R & (R - 1) == 0
    near = range(1, R - 1) if far else range(1, R)
    rd = rows[R - 1]

    def dev(r, c, d):
        return {"row": r, "col": c, "depth": d}

    sib = dev(row, sib_col, dep)

    def zdev(g):
        return dev(row, (g // ND) * 2 + par, g % ND)

    def zrel(g):
        return dev(row, (g // ND) * 2 + 1 - par, g % ND)

    def xdev(j):
        return dev(rows[j], col, dep)

    def xrel(j):
        return dev(rows[j], sib_col, dep)

    def peer(k):
        i = lax.rem(me + k, N)
        g = i // R
        return dev(lax.rem(i, R), (g // ND) * 2 + par, lax.rem(g, ND))

    def rcopy(a, b, ss, rs, to):
        return pltpu.make_async_remote_copy(src_ref=a, dst_ref=b, send_sem=ss, recv_sem=rs,
                                            device_id=to, device_id_type=MESH)

    def each_peer(fn):
        if N <= 32:
            for g in range(G):
                for j in range(R - 1, 0, -1):
                    fn(dev(rows[j], (g // ND) * 2 + par, g % ND))

                @pl.when(grp != g)
                def _(g=g):
                    fn(zdev(g))
        else:
            lax.fori_loop(1, N, lambda k, c: (fn(peer(k)), c)[1], 0)

    def greet(sem, to):
        pl.semaphore_signal(sem, inc=1, device_id=to, device_id_type=MESH)

    barrier = pltpu.get_barrier_semaphore()
    for g in range(G):
        @pl.when(grp != g)
        def _(g=g):
            greet(barrier, zrel(g))
    for j in near:
        greet(barrier, xdev(j))
        greet(barrier, xrel(j))
    if far:
        greet(barrier, xrel(R - 1))
    greet(barrier, sib)
    loads = [pltpu.make_async_copy(a, b, s_in.at[i]) for i, (a, b) in enumerate((
        (src_h, S.at[grp, row]), (tgt_h, tgt), (dual_h, dual_all), (weight_h, weight), (match_h, match_in)))]
    for c in loads:
        c.start()
    for c in loads[:2]:
        c.wait()
    pl.semaphore_wait(barrier, G + 2 * len(near) + (1 if far else 0))

    sends = []

    def go(c):
        c.start()
        sends.append(c)

    mine = S.at[grp, row]

    def z_send(g):
        return rcopy(mine, Q.at[grp], s_z.at[g], r_z.at[grp], zrel(g))

    tour = [jnp.where(grp == 0, G - 1 - k, k) for k in range(G)]
    for g in tour:
        @pl.when(grp != g)
        def _(g=g):
            z_send(g).start()
    if far:
        go(rcopy(mine, QD, s_qd, r_qd, xrel(R - 1)))
    for j in near:
        rcopy(mine, S.at[grp, row], s_x.at[j, grp], r_x.at[row, grp], xdev(j)).start()
    go(rcopy(tgt, T2, s_pair.at[0], r_pair.at[0], sib))
    for j in range(1, R):
        greet(line_in, xrel(j))
    greet(line_in, sib)
    for c in loads[2:]:
        c.wait()
    dual[...] = dual_all[:, pl.ds(pl.multiple_of(row * own, own), own)]
    go(rcopy(dual, dual2, s_pair.at[1], r_pair.at[1], sib))

    for i, vec in ((0, weight[...]), (1, match_in[...].astype(F32))):
        span = ND * n
        for q in range(2):
            parts = [jnp.where(par == q, vec[:, 2 * c * span:(2 * c + 1) * span],
                               vec[:, (2 * c + 1) * span:(2 * c + 2) * span]) for c in range(NC // 2)]
            wm[q, i:i + 1, :] = parts[0] if len(parts) == 1 else jnp.concatenate(parts, axis=1)
    wm_all[row] = wm[0]
    for j in range(1, R):
        go(rcopy(wm.at[1], wm_all.at[row], s_wm.at[j], r_wm.at[row], xrel(j)))

    def x_send(g, j):
        return rcopy(Q.at[g], S.at[g, row], s_x.at[j, g], r_x.at[row, g], sib if j == 0 else xrel(j))

    def d_send(g):
        return rcopy(QD, S.at[grp, rd], s_d.at[g], r_x.at[rd, grp], zrel(g))

    hops = [0] + list(near)
    if far:
        rcopy(QD, QD, s_qd, r_qd, xrel(R - 1)).wait_recv()
        for g in tour:
            d_send(g).start()
    for g in order:
        @pl.when(grp != g)
        def _(g=g):
            rcopy(Q.at[g], Q.at[g], s_z.at[g], r_z.at[g], zrel(g)).wait_recv()
            for j in list(near) + [0]:
                x_send(g, j).start()
    dcol[0:own, :] = jnp.transpose(jnp.broadcast_to(dual[...] * log2e, (128, own)))
    rcopy(dual, dual2, s_pair.at[1], r_pair.at[1], sib).wait_recv()
    dcol[own:2 * own, :] = jnp.transpose(jnp.broadcast_to(dual2[...] * log2e, (128, own)))
    rcopy(tgt, T2, s_pair.at[0], r_pair.at[0], sib).wait_recv()

    lane_rep = C // 128

    def scores_chunk(g):
        block = S[g].reshape(C, D)
        tops = []
        for h, t in ((0, tgt), (1, T2)):
            p = lax.dot_general(t[...], block, (((1,), (1,)), ((), ())), preferred_element_type=F32)
            dc = dcol[h * own:(h + 1) * own, :]
            s = (score_scale * log2e) * p + jnp.concatenate([dc] * lane_rep, axis=1)
            e_buf[g, h * own:(h + 1) * own, :] = s
            tops.append(jnp.max(s, axis=0, keepdims=True))
        top = jnp.maximum(tops[0], tops[1])
        m_buf[g] = top
        e = jnp.exp2(e_buf[g] - top)
        e_buf[g] = e
        lam[g, me] = top + log2e * jnp.log(jnp.sum(e, axis=0, keepdims=True))

    def take(g, r):
        rcopy(S.at[g, r], S.at[g, r], s_x.at[0, 0], r_x.at[r, g], sib).wait_recv()

    place = sum(i * (grp == g).astype(jnp.int32) for i, g in enumerate(order))
    for i in range(G):
        g = grp if i == 0 else jnp.where(place >= i, order[i - 1], order[i])
        for j in range(0 if i else 1, R):
            take(g, rows[j])
        scores_chunk(g)
        if i == 0:
            pl.semaphore_wait(line_in, R)
        each_peer(lambda to: rcopy(lam.at[g, me], lam.at[g, me], s_l.at[g], r_l.at[g], to).start())

    for j in range(1, R):
        rcopy(wm.at[1], wm_all.at[rows[j]], s_wm.at[j], r_wm.at[rows[j]], xrel(j)).wait_recv()
    for g in range(G):
        for i in range(2):
            wm_g[g, i:i + 1, :] = jnp.concatenate(
                [wm_all[r, i:i + 1, g * n:(g + 1) * n] for r in range(R)], axis=1)

    first = [((c * ND + dep) * R + row) * own for c in (col, sib_col)]

    def lam_all(g):
        every = lam.at[g, pl.ds(0, N - 1)]
        return rcopy(every, every, s_l.at[g], r_l.at[g], sib)

    halves = ((0, tgt), (1, T2))
    over_targets = (((0,), (0,)), ((), ()))

    def hits(g, h):
        match = wm_g[g, 1:2, :].astype(jnp.int32)
        return lax.broadcasted_iota(jnp.int32, (own, C), 0) == match - first[h]

    def scale_of(g):
        lam_all(g).wait_recv()
        parts = lam[g]
        peak = jnp.max(parts, axis=0)
        log_total = peak + log2e * jnp.log(jnp.sum(jnp.exp2(parts - peak[None]), axis=0))
        return wm_g[g, 0:1, :] * jnp.exp2(m_buf[g] - log_total)

    def round_delta(g, h, scale):
        hit = jnp.where(hits(g, h), wm_g[g, 0:1, :], 0.0)
        d = (scale * e_buf[g, h * own:(h + 1) * own, :] - hit).astype(BF16)
        dbuf[g, h * own:(h + 1) * own, :] = d
        return d

    def delta_chunk(g):
        scale = scale_of(g)
        part = None
        for h, t in halves:
            q = lax.dot_general(round_delta(g, h, scale), t[...], over_targets, preferred_element_type=F32)
            part = q if part is None else part + q
        return part

    def prepare(g):
        u = k = m = None
        for h, t in halves:
            e = e_buf[g, h * own:(h + 1) * own, :]
            hit = hits(g, h)
            at = jnp.sum(jnp.where(hit, e, 0.0), axis=0, keepdims=True)
            uh = lax.dot_general(jnp.where(hit, 0.0, e).astype(BF16), t[...], over_targets, preferred_element_type=F32)
            kh = lax.dot_general(jnp.where(hit, 1.0, 0.0).astype(BF16), t[...], over_targets, preferred_element_type=F32)
            u, k, m = (uh, kh, at) if h == 0 else (u + uh, k + kh, m + at)
        U[g] = u
        H[g] = k
        em[g] = m

    def prepared(g):
        scale = scale_of(g)
        m_buf[g] = scale
        coef = (scale * em[g] - wm_g[g, 0:1, :]).astype(BF16).astype(F32)

        def down(v):
            return jnp.concatenate([jnp.transpose(jnp.broadcast_to(v, (128, C)))] * (D // 128), axis=1)

        return down(scale) * U[g] + down(coef) * H[g]

    def p_send(g, j):
        apart = (grp != g).astype(jnp.int32)
        to = sib if j == 0 else dev(rows[j], col + apart * (sib_col - col), dep)
        return rcopy(ps.at[g, rows[j]], px.at[g, row], s_p.at[j, g], r_p.at[row, g], to)

    def far_send(g):
        return rcopy(ps.at[g, rd], zd.at[grp], s_zd.at[g], r_zd.at[grp], zrel(g))

    def gt_half(h, groups):
        acc = None
        for g in groups:
            q = jnp.dot(dbuf[g, h * own:(h + 1) * own, :], S[g].reshape(C, D), preferred_element_type=F32)
            acc = q if acc is None else acc + q
        return acc

    early = order
    for g in early:
        prepare(g)

    def taken(g, j):
        rcopy(ps.at[g, rows[j]], px.at[g, rows[j]], s_p.at[j, g], r_p.at[rows[j], g], sib).wait_recv()
        return px[g, rows[j]].astype(F32)

    def zp_send(g):
        return rcopy(zs.at[g], zr.at[grp], s_zp.at[g], r_zp.at[grp], zrel(g))

    def relay(g):
        @pl.when(grp != g)
        def _():
            acc = taken(g, 0)
            for j in near:
                acc = acc + taken(g, j)
            zs[g] = acc.astype(BF16)
            zp_send(g).start()

    for i, g in enumerate(order):
        if i == G - 1 and G > 1:
            gt_send[...] = gt_half(1, order[:-1])
        part = (prepared(g) if g in early else delta_chunk(g)).reshape(R, n, D)
        ps[g] = part.astype(BF16)
        if far:
            far_send(g).start()
        for j in near:
            p_send(g, j).start()

        @pl.when(grp != g)
        def _(g=g):
            p_send(g, 0).start()

        @pl.when(grp == g)
        def _(part=part):
            partf[...] = part

        if g in early:
            for h in range(2):
                round_delta(g, h, m_buf[g])

    last = order[-1:]
    gt_send[...] = gt_send[...] + gt_half(1, last) if G > 1 else gt_half(1, last)
    go(rcopy(gt_send, gt_recv, s_pair.at[2], r_pair.at[2], sib))

    def far_copy():
        return rcopy(ds, dr, s_dr, r_dr, xrel(R - 1))

    def far_relay():
        acc = None
        for g in range(G):
            rcopy(zs.at[g], zd.at[g], s_zd.at[g], r_zd.at[g], sib).wait_recv()
            acc = zd[g].astype(F32) if acc is None else acc + zd[g].astype(F32)
        ds[...] = acc.astype(BF16)
        far_copy().start()

    for i, g in enumerate(order):
        relay(g)
        if far:
            pl.when(grp == g)(far_relay)

    gt_mine = gt_half(0, order)
    rcopy(gt_send, gt_recv, s_pair.at[2], r_pair.at[2], sib).wait_recv()
    gt_out[...] = score_scale * (gt_mine + gt_recv[...])

    acc = partf[row]
    for j in near:
        acc = acc + taken(grp, j)
    gs_out[...] = acc
    for g in order:
        @pl.when(grp != g)
        def _(g=g):
            rcopy(zs.at[g], zr.at[g], s_zp.at[g], r_zp.at[g], sib).wait_recv()
            gs_out[...] = gs_out[...] + zr[g].astype(F32)
    if far:
        far_copy().wait_recv()
        gs_out[...] = score_scale * (gs_out[...] + dr[...].astype(F32))
    else:
        gs_out[...] = score_scale * gs_out[...]

    for c in sends:
        c.wait_send()
    if far:
        far_copy().wait_send()
    for g in range(G):
        lam_all(g).wait_send()
        for j in near:
            x_send(g, j).wait_send()
            p_send(g, j).wait_send()
        if far:
            d_send(g).wait_send()
            far_send(g).wait_send()

        @pl.when(grp != g)
        def _(g=g):
            z_send(g).wait_send()
            x_send(g, 0).wait_send()
            p_send(g, 0).wait_send()
            zp_send(g).wait_send()


def flush(gs, gt, gs_out, gt_out, sem):
    copies = [pltpu.make_async_copy(gt, gt_out, sem.at[0]), pltpu.make_async_copy(gs, gs_out, sem.at[1])]
    for c in copies:
        c.start()
    for c in copies:
        c.wait()


def per_device(R, NC, ND, source_desc, target_desc, target_dual, row_weight, matches):
    n, D = source_desc.shape
    own = target_desc.shape[0]
    G = (NC // 2) * ND
    C = R * n
    vm = pl.BlockSpec(memory_space=pltpu.VMEM)
    dma = pltpu.SemaphoreType.DMA
    outs = pl.pallas_call(
        functools.partial(kernel, R, NC, ND),
        out_shape=(jax.ShapeDtypeStruct((n, D), F32), jax.ShapeDtypeStruct((own, D), F32)),
        in_specs=[pl.BlockSpec(memory_space=pltpu.HBM)] * 5,
        out_specs=(vm, vm),
        scratch_shapes=[
            pltpu.VMEM((own, D), BF16),
            pltpu.VMEM((1, target_dual.shape[0]), F32),
            pltpu.VMEM((1, row_weight.shape[0]), F32),
            pltpu.VMEM((1, row_weight.shape[0]), jnp.int32),
            pltpu.VMEM((G, R, n, D), BF16),
            pltpu.VMEM((G, n, D), BF16),
            pltpu.VMEM((n, D), BF16),
            pltpu.VMEM((own, D), BF16),
            pltpu.VMEM((1, own), F32),
            pltpu.VMEM((1, own), F32),
            pltpu.VMEM((2, 2, G * n), F32),
            pltpu.VMEM((R, 2, G * n), F32),
            pltpu.VMEM((G, 2, C), F32),
            pltpu.VMEM((2 * own, 128), F32),
            pltpu.VMEM((G, 2 * own, C), F32),
            pltpu.VMEM((G, 1, C), F32),
            pltpu.VMEM((G, R * G, 1, C), F32),
            pltpu.VMEM((G, 2 * own, C), BF16),
            pltpu.VMEM((G, C, D), F32),
            pltpu.VMEM((G, C, D), F32),
            pltpu.VMEM((G, 1, C), F32),
            pltpu.VMEM((G, R, n, D), BF16),
            pltpu.VMEM((G, R, n, D), BF16),
            pltpu.VMEM((G, n, D), BF16),
            pltpu.VMEM((G, n, D), BF16),
            pltpu.VMEM((G, n, D), BF16),
            pltpu.VMEM((n, D), BF16),
            pltpu.VMEM((n, D), BF16),
            pltpu.VMEM((R, n, D), F32),
            pltpu.VMEM((own, D), F32),
            pltpu.VMEM((own, D), F32),
            dma((5,)),
            dma((3,)), dma((3,)),
            dma((G,)), dma((G,)),
            dma((R, G)), dma((R, G)),
            dma, dma,
            dma((G,)),
            dma((R,)), dma((R,)),
            dma((G,)), dma((G,)),
            dma((R, G)), dma((R, G)),
            dma((G,)), dma((G,)),
            dma((G,)), dma((G,)),
            dma, dma,
            pltpu.SemaphoreType.REGULAR,
        ],
        compiler_params=pltpu.CompilerParams(collective_id=0, has_side_effects=True,
                                             vmem_limit_bytes=32 * 1024 * 1024),
    )(*[pltpu.with_memory_space_constraint(a, pltpu.HBM) for a in (
        source_desc, target_desc, target_dual[None, :], row_weight[None, :], matches[None, :])])
    hbm = pl.BlockSpec(memory_space=pltpu.HBM)
    return pl.pallas_call(
        flush,
        out_shape=(jax.ShapeDtypeStruct((n, D), F32), jax.ShapeDtypeStruct((own, D), F32)),
        in_specs=[vm, vm],
        out_specs=(hbm, hbm),
        scratch_shapes=[dma((2,))],
        compiler_params=pltpu.CompilerParams(vmem_limit_bytes=8 * 1024 * 1024),
    )(*outs)


def solution(mesh):
    R, NC, ND = mesh.shape["row"], mesh.shape["col"], mesh.shape["depth"]
    return jax.shard_map(
        functools.partial(per_device, R, NC, ND),
        mesh=mesh,
        in_specs=(
            P(("row", "col", "depth"), None),
            P(("col", "depth", "row"), None),
            P(("col", "depth")),
            P("row"),
            P("row"),
        ),
        out_specs=(P(("row", "col", "depth"), None), P(("col", "depth", "row"), None)),
        check_vma=False,
    )
```
